32 devices in a mesh: row: 4 (over y, x), col: 8 (over z, core).
Axes of the slice: x: 2, y: 2, z: 4, core: 2. Of those that a mesh axis runs over, the one named last changes fastest.
Arguments:
- tile_left: bfloat16 [4, 16, 2048, 64], P('row', 'col'), may hold values from -6 to 6
- tile_right: bfloat16 [4, 16, 2048, 64], P('row', 'col'), may hold values from -0.75 to 0.75
- panel_rows: bfloat16 [4, 2048, 128], P('row', 'col'), may hold values from -0.71875 to 0.71875
- panel_cols: bfloat16 [16, 2048, 128], P('col', 'row'), may hold values from -0.71875 to 0.71875
- vectors: bfloat16 [16, 2048, 32], P('col', 'row'), may hold values from -0.033203125 to 0.033203125
- omega: bfloat16 [2048, 64], replicated, may hold values from -0.125 to 0.125
- psi: bfloat16 [2048, 64], replicated, may hold values from -0.125 to 0.125
Outputs:
- sketch_left: bfloat16 [4, 16, 2048, 64], P('row', 'col')
- sketch_right: bfloat16 [4, 16, 2048, 64], P('row', 'col')
- product: float32 [4, 2048, 32], P('row', 'col')
The draws below stay inside these ranges and needn't reach their ends.
All inputs are finite; a program needn't handle non-finite values.
Results may differ from the reference program's by a relative error of at most 0.0049.
Values may be sent and summed in bfloat16 or wider, within the bound.
No kernel may reach another device: no remote copies, remote signals or barrier semaphores. Data moves between devices by JAX's collectives and lax.ppermute only.
A program may use at most 64 MiB of HBM per device.

```python
import jax
import jax.numpy as jnp
from jax import lax

NB = 2048
RANK = 64
NV = 32
NTR = 4
NTC = 16


def levels(key, extent, cuts, low, largest):
    gain = 1.0
    for position, blocks in cuts:
        steps = jax.random.uniform(jax.random.fold_in(jax.random.fold_in(key, 6), position), (blocks,), jnp.float32, low / len(cuts), largest / len(cuts))
        gain = gain * jnp.repeat(jnp.exp(steps), extent[position] // blocks).reshape((-1,) + (1,) * (len(extent) - 1 - position))
    return gain


def bell_draw(own_key, dims, spread, bound, pieces=(), kind=jnp.bfloat16):
    loudness = levels(own_key, dims, pieces, -0.22, 0.18) if pieces else 1.0
    array = jax.random.normal(own_key, dims, jnp.float32) * spread * loudness
    return jnp.minimum(jnp.maximum(array, -bound), bound).astype(kind)


def setup_inputs(seed: int = 0) -> dict:
    streams_of = jax.random.split(jax.random.key(seed), 8)
    tile_left = bell_draw(streams_of[0], (NTR, NTC, NB, RANK), 1.0, 6.0, ((0, 4), (1, 8)))
    tile_right = bell_draw(streams_of[1], (NTR, NTC, NB, RANK), RANK ** -0.5, 0.75, ((0, 4), (1, 8)))
    panel_rows = bell_draw(streams_of[2], (NTR, NB, 2 * RANK), 0.12, 0.71875, ((0, 4), (1, 8)))
    panel_cols = bell_draw(streams_of[3], (NTC, NB, 2 * RANK), 0.12, 0.71875, ((0, 8), (1, 4)))
    vectors = bell_draw(streams_of[4], (NTC, NB, NV), (1.0 / (45.0 * NTC ** 0.5)), 0.033203125, ((0, 8), (1, 4)))
    omega = bell_draw(streams_of[5], (NB, RANK), NB ** -0.5, 0.125)
    psi = bell_draw(streams_of[6], (NB, RANK), NB ** -0.5, 0.125)
    return dict(tile_left=tile_left, tile_right=tile_right, panel_rows=panel_rows, panel_cols=panel_cols, vectors=vectors, omega=omega, psi=psi)


def reference(tile_left, tile_right, panel_rows, panel_cols, vectors, omega, psi):
    col_left = panel_cols[:, :, :RANK]
    col_right = panel_cols[:, :, RANK:]
    hi = lax.Precision.HIGHEST
    col_sketch = jnp.einsum('tnk,nl->tkl', col_left, omega, preferred_element_type=jnp.float32)
    vec_proj = jnp.einsum('tnk,tnv->tkv', col_left, vectors, preferred_element_type=jnp.float32)

    def one_row(items):
        left_t, right_t, prow = items
        row_left = prow[:, :RANK]
        row_right = prow[:, RANK:]
        gram_mat = jnp.einsum('nk,tnl->tkl', row_right, col_right, preferred_element_type=jnp.float32)
        coef_a = jnp.einsum('tnk,nl->tkl', right_t, omega, preferred_element_type=jnp.float32).astype(jnp.bfloat16)
        coef_b = jnp.einsum('tkm,tml->tkl', gram_mat, col_sketch, precision=hi).astype(jnp.bfloat16)
        first = jnp.einsum('tnk,tkl->tnl', left_t, coef_a, preferred_element_type=jnp.float32)
        first = first - jnp.einsum('nk,tkl->tnl', row_left, coef_b, preferred_element_type=jnp.float32)
        coef_c = jnp.einsum('tnk,nl->tkl', left_t, psi, preferred_element_type=jnp.float32).astype(jnp.bfloat16)
        row_sketch = jnp.dot(row_left.T, psi, preferred_element_type=jnp.float32)
        coef_d = jnp.einsum('tmk,ml->tkl', gram_mat, row_sketch, precision=hi).astype(jnp.bfloat16)
        second = jnp.einsum('tnk,tkl->tnl', right_t, coef_c, preferred_element_type=jnp.float32)
        second = second - jnp.einsum('tnk,tkl->tnl', col_left, coef_d, preferred_element_type=jnp.float32)
        coef_p = jnp.einsum('tnk,tnv->tkv', right_t, vectors, preferred_element_type=jnp.float32).astype(jnp.bfloat16)
        coef_q = jnp.einsum('tkm,tmv->tkv', gram_mat, vec_proj, precision=hi).astype(jnp.bfloat16)
        summed = jnp.einsum('tnk,tkv->nv', left_t, coef_p, preferred_element_type=jnp.float32)
        summed = summed - jnp.einsum('nk,tkv->nv', row_left, coef_q, preferred_element_type=jnp.float32)
        return first.astype(jnp.bfloat16), second.astype(jnp.bfloat16), summed

    sketch_left, sketch_right, product = lax.map(one_row, (tile_left, tile_right, panel_rows))
    return sketch_left, sketch_right, product
```

```python
import functools

import jax
import jax.numpy as jnp
from jax import lax
from jax.experimental import pallas as pl
from jax.experimental.pallas import tpu as pltpu
from jax.sharding import PartitionSpec as P


F32 = jnp.float32
BF16 = jnp.bfloat16
HI = lax.Precision.HIGHEST


def nn(a, b, precision=None):
    return lax.dot_general(
        a, b, (((1,), (0,)), ((), ())), precision=precision, preferred_element_type=F32
    )


def nt(a, b, precision=None):
    return lax.dot_general(
        a, b, (((1,), (1,)), ((), ())), precision=precision, preferred_element_type=F32
    )


def vmem_call(kernel, out_shape, *args, scratch=()):
    vm = pl.BlockSpec(memory_space=pltpu.VMEM)
    outs = jax.tree.map(lambda _: vm, out_shape)
    return pl.pallas_call(
        kernel,
        out_shape=out_shape,
        in_specs=[vm] * len(args),
        out_specs=outs,
        scratch_shapes=list(scratch),
    )(*args)


def shape(dims, dtype):
    return jax.ShapeDtypeStruct(dims, dtype)


def pack_kernel(tiles, rank, cols_ref, vec_ref, u_ref, v_ref, proj_ref):
    u = jnp.concatenate([cols_ref[t, :, :rank] for t in range(tiles)], axis=1)
    v = jnp.concatenate([cols_ref[t, :, rank:] for t in range(tiles)], axis=1)
    u_ref[...] = u
    v_ref[...] = v
    part = [nn(vec_ref[t], u[:, t * rank : (t + 1) * rank]) for t in range(tiles)]
    proj_ref[...] = jnp.concatenate(part, axis=1)


def local_kernel(tiles, rank, parts, *refs):
    left, right, omega, psi = refs[:4]
    vecs = refs[4 : 4 + parts]
    first, second, term = refs[4 + parts :]
    chunk = vecs[0].shape[2]
    row = lax.axis_index("row")
    total = None
    for t in range(tiles):
        coef_a = nt(omega[...], right[t]).astype(BF16)
        coef_c = nt(psi[...], left[t]).astype(BF16)
        coef_p = None
        for k in range(parts):
            at = pl.ds(pl.multiple_of((row ^ k) * chunk, chunk), chunk)
            part = nt(vecs[k][t], right[t, :, at])
            coef_p = part if coef_p is None else coef_p + part
        both = nn(jnp.concatenate([coef_a, coef_p.astype(BF16)], axis=0), left[t])
        first[t] = both[:rank]
        total = both[rank:] if total is None else total + both[rank:]
        second[t] = nn(coef_c, right[t])
    term[...] = total


def gram_kernel(tiles, rank, rparts, cparts, split, *refs):
    psi, term = refs[:2]
    rows = refs[2 : 2 + cparts]
    vs = refs[2 + cparts : 2 + cparts + rparts]
    projs = refs[2 + cparts + rparts : 2 + cparts + 2 * rparts]
    gram_out, coef_d_out, rows_full = refs[2 + cparts + 2 * rparts : 5 + cparts + 2 * rparts]
    rest = refs[5 + cparts + 2 * rparts :]
    row, col = lax.axis_index("row"), lax.axis_index("col")
    size = rows[0].shape[0]
    for m in range(cparts):
        at = pl.ds(pl.multiple_of((col ^ m) * size, size), size)
        rows_full[at, :] = rows[m][...]
    chunk = vs[0].shape[0]
    gram = None
    for k in range(rparts):
        at = pl.ds(pl.multiple_of((row ^ k) * chunk, chunk), chunk)
        part = lax.dot_general(
            rows_full[at, :], vs[k][...], (((0,), (0,)), ((), ())), preferred_element_type=F32
        )
        gram = part if gram is None else gram + part
    gram = gram[rank:, :]
    gram_out[...] = gram
    row_sketch = nn(psi[...], rows_full[...])[:, :rank]
    coef_d_out[...] = nn(row_sketch, gram, HI).astype(BF16)
    proj = functools.reduce(lambda a, b: a + b, [p[...] for p in projs])
    coef_q = nt(proj, gram, HI).astype(BF16)
    padded = jnp.concatenate([coef_q, jnp.zeros_like(coef_q)], axis=1)
    total = term[...] - nt(padded, rows_full[...])
    if split:
        keep, send, full = rest
        full[...] = total
        for m in range(cparts // 2):
            at = pl.ds(pl.multiple_of((col ^ (2 * m)) * size, size), size)
            keep[m] = full[:, at]
            at = pl.ds(pl.multiple_of((col ^ (2 * m + 1)) * size, size), size)
            send[m] = full[:, at].astype(BF16)
    else:
        rest[0][...] = total


def final_kernel(tiles, rank, parts, *refs):
    first, second, omega, gram, coef_d, rows_full = refs[:6]
    us = refs[6 : 6 + parts]
    out_first, out_second = refs[6 + parts :]
    row = lax.axis_index("row")
    chunk = us[0].shape[0]
    lane = lax.broadcasted_iota(jnp.int32, (omega.shape[0], tiles * rank), 1)
    sketch = None
    for k in range(parts):
        at = pl.ds(pl.multiple_of((row ^ k) * chunk, chunk), chunk)
        part = nn(omega[:, at], us[k][...])
        sketch = part if sketch is None else sketch + part
    gram_all = gram[...]
    lows, ds = [], []
    for t in range(tiles):
        mine = (lane >= t * rank) & (lane < (t + 1) * rank)
        coef_b = nt(jnp.where(mine, sketch, 0.0), gram_all, HI).astype(BF16)
        lows.append(jnp.concatenate([coef_b, jnp.zeros_like(coef_b)], axis=1))
        ds.append(jnp.where(mine, coef_d[...].astype(F32), 0.0).astype(BF16))
    width = omega.shape[0]
    part = nt(jnp.concatenate(lows, axis=0), rows_full[...])
    for t in range(tiles):
        out_first[t] = (first[t] - part[t * width : (t + 1) * width]).astype(BF16)
    coefs = jnp.concatenate(ds, axis=0)
    for k in range(parts):
        at = pl.ds(pl.multiple_of((row ^ k) * chunk, chunk), chunk)
        part = nt(coefs, us[k][...])
        for t in range(tiles):
            out_second[t, :, at] = (second[t, :, at] - part[t * width : (t + 1) * width]).astype(BF16)


def local(n_row, n_col, tile_left, tile_right, panel_rows, panel_cols, vectors, omega, psi):
    tiles, order, rank = tile_left.shape[1:]
    nvec = vectors.shape[2]
    chunk = panel_cols.shape[1]
    size = panel_rows.shape[1]
    wide = omega.shape[1]

    def swap(name, count, value, m):
        return lax.ppermute(value, name, [(i, i ^ m) for i in range(count)])

    left = jnp.swapaxes(tile_left[0], 1, 2)
    right = jnp.swapaxes(tile_right[0], 1, 2)
    vec = jnp.swapaxes(vectors, 1, 2)
    omega_t, psi_t = omega.T, psi.T
    rows = panel_rows[0]

    u, v, proj = vmem_call(
        functools.partial(pack_kernel, tiles, rank),
        (
            shape((chunk, tiles * rank), BF16),
            shape((chunk, tiles * rank), BF16),
            shape((nvec, tiles * rank), F32),
        ),
        panel_cols,
        vec,
    )
    row_swap = functools.partial(swap, "row", n_row)
    col_swap = functools.partial(swap, "col", n_col)
    vs = [v] + [row_swap(v, k) for k in range(1, n_row)]
    xs = [vec] + [row_swap(vec, k) for k in range(1, n_row)]
    projs = [proj] + [row_swap(proj, k) for k in range(1, n_row)]
    us = [u] + [row_swap(u, k) for k in range(1, n_row)]
    same = [rows] + [col_swap(rows, 2 * m) for m in range(1, n_col // 2)]
    other = [col_swap(x, 1) for x in same]
    row_parts = [x for pair in zip(same, other) for x in pair]

    first, second, term = vmem_call(
        functools.partial(local_kernel, tiles, rank, n_row),
        (
            shape((tiles, wide, order), F32),
            shape((tiles, wide, order), F32),
            shape((nvec, order), F32),
        ),
        left,
        right,
        omega_t,
        psi_t,
        *xs,
    )
    split = size % 128 == 0
    half = n_col // 2
    outs = (
        shape((rank, tiles * rank), F32),
        shape((wide, tiles * rank), BF16),
        shape((order, 2 * rank), BF16),
    )
    if split:
        outs += (shape((half, nvec, size), F32), shape((half, nvec, size), BF16))
    else:
        outs += (shape((nvec, order), F32),)
    gram, coef_d, rows_full, *rest = vmem_call(
        functools.partial(gram_kernel, tiles, rank, n_row, n_col, split),
        outs,
        psi_t,
        term,
        *row_parts,
        *vs,
        *projs,
        scratch=[pltpu.VMEM((nvec, order), F32)] if split else [],
    )
    if split:
        keep, send = rest
    else:
        col = lax.axis_index("col")
        blocks = rest[0].reshape(nvec, n_col, size).swapaxes(0, 1)
        where = col ^ (2 * jnp.arange(half))
        keep = blocks[where]
        send = blocks[where ^ 1].astype(BF16)
    got = col_swap(send, 1)
    mine = keep[0] + got[0].astype(F32)
    arrived = [
        col_swap((keep[m] + got[m].astype(F32)).astype(BF16), 2 * m) for m in range(1, half)
    ]
    out_first, out_second = vmem_call(
        functools.partial(final_kernel, tiles, rank, n_row),
        (shape((tiles, wide, order), BF16), shape((tiles, wide, order), BF16)),
        first,
        second,
        omega_t,
        gram,
        coef_d,
        rows_full,
        *us,
    )
    for x in arrived:
        mine = mine + x.astype(F32)
    return (
        jnp.swapaxes(out_first, 1, 2)[None],
        jnp.swapaxes(out_second, 1, 2)[None],
        mine.T[None],
    )


def solution(mesh):
    in_specs = (
        P("row", "col", None, None),
        P("row", "col", None, None),
        P("row", "col", None),
        P("col", "row", None),
        P("col", "row", None),
        P(),
        P(),
    )
    out_specs = (P("row", "col", None, None), P("row", "col", None, None), P("row", "col", None))
    body = functools.partial(local, mesh.shape["row"], mesh.shape["col"])
    return jax.shard_map(body, mesh=mesh, in_specs=in_specs, out_specs=out_specs, check_vma=False)
```

```python
import functools

import jax
import jax.numpy as jnp
from jax import lax
from jax.experimental import pallas as pl
from jax.experimental.pallas import tpu as pltpu
from jax.sharding import PartitionSpec as P


F32 = jnp.float32
BF16 = jnp.bfloat16
HI = lax.Precision.HIGHEST
LANES = 128


def nn(a, b, precision=None):
    return lax.dot_general(
        a, b, (((1,), (0,)), ((), ())), precision=precision, preferred_element_type=F32
    )


def nt(a, b, precision=None):
    return lax.dot_general(
        a, b, (((1,), (1,)), ((), ())), precision=precision, preferred_element_type=F32
    )


def tn(a, b):
    return lax.dot_general(a, b, (((0,), (0,)), ((), ())), preferred_element_type=F32)


def call(kernel, out_shape, *args, scratch=(), resident=True):
    vm = pl.BlockSpec(memory_space=pltpu.VMEM)
    space = pltpu.VMEM if resident else pltpu.HBM
    args = [pltpu.with_memory_space_constraint(x, space) for x in args]
    return pl.pallas_call(
        kernel,
        out_shape=out_shape,
        in_specs=[vm] * len(args),
        out_specs=jax.tree.map(lambda _: vm, out_shape),
        scratch_shapes=list(scratch),
        compiler_params=pltpu.CompilerParams(vmem_limit_bytes=16 << 20),
    )(*args)


def add_all(xs):
    return functools.reduce(lambda a, b: a + b, xs)


def at_block(index, size):
    return pl.ds(pl.multiple_of(index * size, size), size)


def pack_kernel(tiles, rank, cols_ref, vec_ref, u_ref, v_ref):
    chunk, nvec = cols_ref.shape[1], vec_ref.shape[1]
    u = jnp.concatenate([cols_ref[t, :, :rank] for t in range(tiles)], axis=1)
    u_ref[...] = u
    v_ref[:chunk] = jnp.concatenate([cols_ref[t, :, rank:] for t in range(tiles)], axis=1)
    part = [nn(vec_ref[t], u[:, t * rank : (t + 1) * rank]) for t in range(tiles)]
    base = chunk
    for b in range(chunk // LANES):
        for t in range(tiles):
            v_ref[base : base + nvec] = vec_ref[t, :, b * LANES : (b + 1) * LANES]
            base += nvec
    v_ref[base:] = jnp.concatenate(part, axis=1).astype(BF16)


def local_kernel(tiles, left, right, omega, psi, first, second, left_o, right_o, omega_o, psi_o):
    for t in range(tiles):
        coef_a = nt(omega[...], right[t]).astype(BF16)
        coef_c = nt(psi[...], left[t]).astype(BF16)
        first[t] = nn(coef_a, left[t])
        second[t] = nn(coef_c, right[t])
    left_o[...] = left[...]
    right_o[...] = right[...]
    omega_o[...] = omega[...]
    psi_o[...] = psi[...]


def gram_kernel(tiles, rank, nvec, rparts, cparts, split, *refs):
    left, right, psi = refs[:3]
    rows = refs[3 : 3 + cparts]
    vs = refs[3 + cparts : 3 + cparts + rparts]
    gram_out, coef_d_out, rows_full = refs[3 + cparts + rparts : 6 + cparts + rparts]
    rest, vec_full = refs[6 + cparts + rparts : -1], refs[-1]
    row, col = lax.axis_index("row"), lax.axis_index("col")
    size = rows[0].shape[0]
    for m in range(cparts):
        rows_full[at_block(col ^ m, size), :] = rows[m][...]
    chunk = left.shape[2] // rparts
    blocks = chunk // LANES
    wide = tiles * nvec
    for k in range(rparts):
        for b in range(blocks):
            at = chunk + b * wide
            vec_full[:, at_block((row ^ k) * blocks + b, LANES)] = vs[k][at : at + wide]
    gram = add_all(
        [tn(rows_full[at_block(row ^ k, chunk), :], vs[k][:chunk]) for k in range(rparts)]
    )[rank:, :]
    gram_out[...] = gram
    row_sketch = nn(psi[...], rows_full[...])[:, :rank]
    coef_d_out[...] = nn(row_sketch, gram, HI).astype(BF16)
    proj = add_all([v[chunk + blocks * wide :].astype(F32) for v in vs])
    coef_q = nt(proj, gram, HI).astype(BF16)
    padded = jnp.concatenate([coef_q, jnp.zeros_like(coef_q)], axis=1)
    total = -nt(padded, rows_full[...])
    for t in range(tiles):
        coef_p = nt(vec_full[t * nvec : (t + 1) * nvec], right[t]).astype(BF16)
        total = total + nn(coef_p, left[t])
    if split:
        keep, send, full = rest
        full[...] = total
        for m in range(cparts // 2):
            keep[m] = full[:, at_block(col ^ (2 * m), size)]
            send[m] = full[:, at_block(col ^ (2 * m + 1), size)].astype(BF16)
    else:
        rest[0][...] = total


def final_kernel(tiles, rank, parts, *refs):
    first, second, omega, gram, coef_d, rows_full = refs[:6]
    us = refs[6 : 6 + parts]
    out_first, out_second = refs[6 + parts :]
    row = lax.axis_index("row")
    chunk = us[0].shape[0]
    width = omega.shape[0]
    lane = lax.broadcasted_iota(jnp.int32, (width, tiles * rank), 1)
    sketch = add_all(
        [nn(omega[:, at_block(row ^ k, chunk)], us[k][...]) for k in range(parts)]
    )
    gram_all = gram[...]
    lows, ds = [], []
    for t in range(tiles):
        mine = (lane >= t * rank) & (lane < (t + 1) * rank)
        coef_b = nt(jnp.where(mine, sketch, 0.0), gram_all, HI).astype(BF16)
        lows.append(jnp.concatenate([coef_b, jnp.zeros_like(coef_b)], axis=1))
        ds.append(jnp.where(mine, coef_d[...].astype(F32), 0.0).astype(BF16))
    part = nt(jnp.concatenate(lows, axis=0), rows_full[...])
    for t in range(tiles):
        out_first[t] = (first[t] - part[t * width : (t + 1) * width]).astype(BF16)
    coefs = jnp.concatenate(ds, axis=0)
    for k in range(parts):
        at = at_block(row ^ k, chunk)
        part = nt(coefs, us[k][...])
        for t in range(tiles):
            low = part[t * width : (t + 1) * width]
            out_second[t, :, at] = (second[t, :, at] - low).astype(BF16)


def local(n_row, n_col, tile_left, tile_right, panel_rows, panel_cols, vectors, omega, psi):
    tiles, order, rank = tile_left.shape[1:]
    nvec = vectors.shape[2]
    chunk = panel_cols.shape[1]
    size = panel_rows.shape[1]
    wide = omega.shape[1]
    half = n_col // 2

    def swap(axis, count, value, m):
        return lax.ppermute(value, axis, [(i, i ^ m) for i in range(count)])

    def row_swap(value, m):
        return swap("row", n_row, value, m)

    def col_swap(value, m):
        return swap("col", n_col, value, m)

    left = jnp.swapaxes(tile_left[0], 1, 2)
    right = jnp.swapaxes(tile_right[0], 1, 2)
    vec = jnp.swapaxes(vectors, 1, 2)
    omega_t, psi_t = omega.T, psi.T
    rows = panel_rows[0]
    vmem = pltpu.VMEM

    u, v = call(
        functools.partial(pack_kernel, tiles, rank),
        (
            vmem((chunk, tiles * rank), BF16),
            vmem((chunk + tiles * nvec * chunk // LANES + nvec, tiles * rank), BF16),
        ),
        panel_cols,
        vec,
        resident=False,
    )
    vs = [v] + [row_swap(v, k) for k in range(1, n_row)]
    us = [u] + [row_swap(u, k) for k in range(1, n_row)]
    same = [rows] + [col_swap(rows, m) for m in range(2, n_col, 2)]
    other = []
    for x in same:
        other.append(lax.ppermute(x, "col", [(i, i ^ 1) for i in range(n_col)]))
    row_parts = [x for pair in zip(same, other) for x in pair]

    first, second, left, right, omega_t, psi_t = call(
        functools.partial(local_kernel, tiles),
        (
            vmem((tiles, wide, order), F32),
            vmem((tiles, wide, order), F32),
            vmem(left.shape, BF16),
            vmem(right.shape, BF16),
            vmem(omega_t.shape, BF16),
            vmem(psi_t.shape, BF16),
        ),
        left,
        right,
        omega_t,
        psi_t,
        resident=False,
    )
    split = size % LANES == 0
    outs = (
        vmem((rank, tiles * rank), F32),
        vmem((wide, tiles * rank), BF16),
        vmem((order, 2 * rank), BF16),
    )
    if split:
        outs += (vmem((half, nvec, size), F32), vmem((half, nvec, size), BF16))
    else:
        outs += (vmem((nvec, order), F32),)
    scratch = [pltpu.VMEM((tiles * nvec, order), BF16)]
    gram, coef_d, rows_full, *rest = call(
        functools.partial(gram_kernel, tiles, rank, nvec, n_row, n_col, split),
        outs,
        left,
        right,
        psi_t,
        *row_parts,
        *vs,
        scratch=([pltpu.VMEM((nvec, order), F32)] if split else []) + scratch,
    )
    if split:
        keep, send = rest
    else:
        col = lax.axis_index("col")
        blocks = rest[0].reshape(nvec, n_col, size).swapaxes(0, 1)
        where = col ^ (2 * jnp.arange(half))
        keep = blocks[where]
        send = blocks[where ^ 1].astype(BF16)
    got = col_swap(send, 1)
    mine = keep[0] + got[0].astype(F32)
    arrived = [col_swap((keep[m] + got[m].astype(F32)).astype(BF16), 2 * m) for m in range(1, half)]
    out_first, out_second = call(
        functools.partial(final_kernel, tiles, rank, n_row),
        (
            jax.ShapeDtypeStruct((tiles, wide, order), BF16),
            jax.ShapeDtypeStruct((tiles, wide, order), BF16),
        ),
        first,
        second,
        omega_t,
        gram,
        coef_d,
        rows_full,
        *us,
    )
    for x in arrived:
        mine = mine + x.astype(F32)
    return (
        jnp.swapaxes(out_first, 1, 2)[None],
        jnp.swapaxes(out_second, 1, 2)[None],
        mine.T[None],
    )


def solution(mesh):
    in_specs = (
        P("row", "col", None, None),
        P("row", "col", None, None),
        P("row", "col", None),
        P("col", "row", None),
        P("col", "row", None),
        P(),
        P(),
    )
    out_specs = (P("row", "col", None, None), P("row", "col", None, None), P("row", "col", None))
    n_row, n_col = mesh.shape["row"], mesh.shape["col"]

    def body(*args):
        return local(n_row, n_col, *args)

    return jax.shard_map(body, mesh=mesh, in_specs=in_specs, out_specs=out_specs, check_vma=False)
```

```python
import functools

import jax
import jax.numpy as jnp
from jax import lax
from jax.experimental import pallas as pl
from jax.experimental.pallas import tpu as pltpu
from jax.sharding import PartitionSpec as P


F32 = jnp.float32
BF16 = jnp.bfloat16
HI = lax.Precision.HIGHEST
LANES = 128


def nn(a, b, precision=None):
    return lax.dot_general(
        a, b, (((1,), (0,)), ((), ())), precision=precision, preferred_element_type=F32
    )


def nt(a, b, precision=None):
    return lax.dot_general(
        a, b, (((1,), (1,)), ((), ())), precision=precision, preferred_element_type=F32
    )


def tn(a, b):
    return lax.dot_general(a, b, (((0,), (0,)), ((), ())), preferred_element_type=F32)


def call(kernel, out_shape, *args, hbm=(), raw=(), scratch=()):
    vm, anywhere = pl.BlockSpec(memory_space=pltpu.VMEM), pl.BlockSpec(memory_space=pl.ANY)
    spaces = [pltpu.HBM if k in hbm or k in raw else pltpu.VMEM for k in range(len(args))]
    args = [pltpu.with_memory_space_constraint(x, space) for x, space in zip(args, spaces)]
    return pl.pallas_call(
        kernel,
        out_shape=out_shape,
        in_specs=[anywhere if k in raw else vm for k in range(len(args))],
        out_specs=jax.tree.map(lambda _: vm, out_shape),
        scratch_shapes=list(scratch),
        compiler_params=pltpu.CompilerParams(vmem_limit_bytes=16 << 20),
    )(*args)


def add_all(xs):
    return functools.reduce(lambda a, b: a + b, xs)


def at_block(index, size):
    return pl.ds(pl.multiple_of(index * size, size), size)


def pack_kernel(tiles, rank, cols_ref, vec_ref, u_ref, v_ref):
    chunk, nvec = cols_ref.shape[1], vec_ref.shape[1]
    u = jnp.concatenate([cols_ref[t, :, :rank] for t in range(tiles)], axis=1)
    u_ref[...] = u
    v_ref[:chunk] = jnp.concatenate([cols_ref[t, :, rank:] for t in range(tiles)], axis=1)
    part = nn(vec_ref[...].reshape(tiles * nvec, chunk), u)
    base = chunk
    for b in range(chunk // LANES):
        for t in range(tiles):
            v_ref[base : base + nvec] = vec_ref[t, :, b * LANES : (b + 1) * LANES]
            base += nvec
    part = [part[t * nvec : (t + 1) * nvec, t * rank : (t + 1) * rank] for t in range(tiles)]
    v_ref[base:] = jnp.concatenate(part, axis=1).astype(BF16)


def load_kernel(tiles, *refs):
    sources, targets, (coef_a, coef_c), sems = refs[:4], refs[4:8], refs[8:10], refs[10]
    copies = [
        pltpu.make_async_copy(s, t, sems.at[k]) for k, (s, t) in enumerate(zip(sources, targets))
    ]
    for copy in copies:
        copy.start()
    for copy in copies:
        copy.wait()
    left, right, omega, psi = targets
    for t in range(tiles):
        coef_a[t] = nt(omega[...], right[t]).astype(BF16)
        coef_c[t] = nt(psi[...], left[t]).astype(BF16)


def pair_kernel(own, other, both):
    size = own.shape[0]
    core = lax.axis_index("col") & 1
    both[at_block(core, size), :] = own[...]
    both[at_block(1 - core, size), :] = other[...]


def gram_kernel(tiles, rank, nvec, rparts, cparts, split, ways, *refs):
    left, right = refs[:2]
    rows, refs = refs[2 : 3 + 2 * len(ways)], refs[3 + 2 * len(ways) :]
    vs, gram_out, rows_full = refs[:rparts], refs[rparts], refs[rparts + 1]
    rest, vec_full = refs[rparts + 2 : -1], refs[-1]
    row, col = lax.axis_index("row"), lax.axis_index("col")
    size = rows_full.shape[0] // cparts
    core, chip = col & 1, col >> 1
    rows_full[at_block(chip, 2 * size), :] = rows[0][...]
    for (one, two), mine, other in zip(ways, rows[1::2], rows[2::2]):
        if one == two:
            at = 2 * (chip ^ one)
            rows_full[at_block(at + core, size), :] = mine[...]
            rows_full[at_block(at + 1 - core, size), :] = other[...]
        else:
            rows_full[at_block(chip ^ (one + core * (two - one)), 2 * size), :] = mine[...]
            rows_full[at_block(chip ^ (two + core * (one - two)), 2 * size), :] = other[...]
    chunk = left.shape[2] // rparts
    blocks = chunk // LANES
    wide = tiles * nvec
    for k in range(rparts):
        for b in range(blocks):
            at = chunk + b * wide
            vec_full[:, at_block((row ^ k) * blocks + b, LANES)] = vs[k][at : at + wide]
    gram = add_all(
        [tn(rows_full[at_block(row ^ k, chunk), :], vs[k][:chunk]) for k in range(rparts)]
    )[rank:, :]
    gram_out[...] = gram
    coef_p = [
        nt(vec_full[t * nvec : (t + 1) * nvec], right[t]).astype(BF16) for t in range(tiles)
    ]
    total = add_all([nn(coef_p[t], left[t]) for t in range(tiles)])
    proj = add_all([v[chunk + blocks * wide :].astype(F32) for v in vs])
    coef_q = nt(proj, gram, HI).astype(BF16)
    padded = jnp.concatenate([coef_q, jnp.zeros_like(coef_q)], axis=1)
    total = total - nt(padded, rows_full[...])
    if split:
        keep, send, full = rest
        full[...] = total
        for m in range(cparts // 2):
            keep[m] = full[:, at_block(col ^ (2 * m), size)]
            send[m] = full[:, at_block(col ^ (2 * m + 1), size)].astype(BF16)
    else:
        rest[0][...] = total


def final_kernel(tiles, rank, parts, *refs):
    left, right, omega, psi, coef_a, coef_c, gram, rows_full = refs[:8]
    us = refs[8 : 8 + parts]
    out_first, out_second = refs[8 + parts :]
    row = lax.axis_index("row")
    chunk = us[0].shape[0]
    width = omega.shape[0]
    lane = lax.broadcasted_iota(jnp.int32, (width, tiles * rank), 1)
    gram_all = gram[...]
    row_sketch = nn(psi[...], rows_full[...])[:, :rank]
    coef_d = nn(row_sketch, gram_all, HI)
    sketch = add_all(
        [nn(omega[:, at_block(row ^ k, chunk)], us[k][...]) for k in range(parts)]
    )
    lows, ds = [], []
    for t in range(tiles):
        mine = (lane >= t * rank) & (lane < (t + 1) * rank)
        coef_b = nt(jnp.where(mine, sketch, 0.0), gram_all, HI).astype(BF16)
        lows.append(jnp.concatenate([coef_b, jnp.zeros_like(coef_b)], axis=1))
        ds.append(jnp.where(mine, coef_d, 0.0).astype(BF16))
    low = nt(jnp.concatenate(lows, axis=0), rows_full[...])
    for t in range(tiles):
        first = nn(coef_a[t], left[t])
        out_first[t] = (first - low[t * width : (t + 1) * width]).astype(BF16)
    coefs = jnp.concatenate(ds, axis=0)
    for k in range(parts):
        at = at_block(row ^ k, chunk)
        low = nt(coefs, us[k][...])
        for t in range(tiles):
            second = nn(coef_c[t], right[t, :, at])
            out_second[t, :, at] = (second - low[t * width : (t + 1) * width]).astype(BF16)


def routes(n_col):
    far = list(range(n_col // 2 - 1, 0, -1))
    return [(far[0], far[0])] * (len(far) % 2) + list(
        zip(far[len(far) % 2 :: 2], far[len(far) % 2 + 1 :: 2])
    )


def local(n_row, n_col, tile_left, tile_right, panel_rows, panel_cols, vectors, omega, psi):
    tiles, order, rank = tile_left.shape[1:]
    nvec = vectors.shape[2]
    chunk = panel_cols.shape[1]
    size = panel_rows.shape[1]
    wide = omega.shape[1]
    half = n_col // 2

    def swap(axis, count, value, m):
        return lax.ppermute(value, axis, [(i, i ^ m) for i in range(count)])

    def row_swap(value, m):
        return swap("row", n_row, value, m)

    def col_swap(value, m):
        return swap("col", n_col, value, m)

    left = jnp.swapaxes(tile_left[0], 1, 2)
    right = jnp.swapaxes(tile_right[0], 1, 2)
    vec = jnp.swapaxes(vectors, 1, 2)
    omega_t, psi_t = omega.T, psi.T
    rows = panel_rows[0]
    vmem = pltpu.VMEM

    u, v = call(
        functools.partial(pack_kernel, tiles, rank),
        (
            vmem((chunk, tiles * rank), BF16),
            vmem((chunk + tiles * nvec * chunk // LANES + nvec, tiles * rank), BF16),
        ),
        panel_cols,
        vec,
        hbm=(0, 1),
    )
    sources = (left, right, omega_t, psi_t)
    left, right, omega_t, psi_t, coef_a, coef_c = call(
        functools.partial(load_kernel, tiles),
        tuple(vmem(x.shape, BF16) for x in sources)
        + (vmem((tiles, wide, rank), BF16), vmem((tiles, wide, rank), BF16)),
        *sources,
        raw=(0, 1, 2, 3),
        scratch=[pltpu.SemaphoreType.DMA((4,))],
    )
    vs = [v] + [row_swap(v, k) for k in range(1, n_row)]
    us = [u] + [row_swap(u, k) for k in range(1, n_row)]
    both = call(pair_kernel, vmem((2 * size, 2 * rank), BF16), rows, col_swap(rows, 1))
    ways = routes(n_col)
    row_parts = [both]
    for one, two in ways:
        perm = [(i, i ^ (2 * (two if i % 2 else one))) for i in range(n_col)]
        got = lax.ppermute(rows if one == two else both, "col", perm)
        row_parts += [got, col_swap(got, 1)]

    split = size % LANES == 0
    outs = (
        vmem((rank, tiles * rank), F32),
        vmem((order, 2 * rank), BF16),
    )
    if split:
        outs += (vmem((half, nvec, size), F32), vmem((half, nvec, size), BF16))
    else:
        outs += (vmem((nvec, order), F32),)
    scratch = [pltpu.VMEM((tiles * nvec, order), BF16)]
    gram, rows_full, *rest = call(
        functools.partial(gram_kernel, tiles, rank, nvec, n_row, n_col, split, ways),
        outs,
        left,
        right,
        *row_parts,
        *vs,
        scratch=([pltpu.VMEM((nvec, order), F32)] if split else []) + scratch,
    )
    if split:
        keep, send = rest
    else:
        col = lax.axis_index("col")
        blocks = rest[0].reshape(nvec, n_col, size).swapaxes(0, 1)
        where = col ^ (2 * jnp.arange(half))
        keep = blocks[where]
        send = blocks[where ^ 1].astype(BF16)
    got = col_swap(send, 1)
    mine = keep[0] + got[0].astype(F32)
    arrived = [col_swap((keep[m] + got[m].astype(F32)).astype(BF16), 2 * m) for m in range(1, half)]
    out_first, out_second = call(
        functools.partial(final_kernel, tiles, rank, n_row),
        (
            jax.ShapeDtypeStruct((tiles, wide, order), BF16),
            jax.ShapeDtypeStruct((tiles, wide, order), BF16),
        ),
        left,
        right,
        omega_t,
        psi_t,
        coef_a,
        coef_c,
        gram,
        rows_full,
        *us,
    )
    for x in arrived:
        mine = mine + x.astype(F32)
    return (
        jnp.swapaxes(out_first, 1, 2)[None],
        jnp.swapaxes(out_second, 1, 2)[None],
        mine.T[None],
    )


def solution(mesh):
    in_specs = (
        P("row", "col", None, None),
        P("row", "col", None, None),
        P("row", "col", None),
        P("col", "row", None),
        P("col", "row", None),
        P(),
        P(),
    )
    out_specs = (P("row", "col", None, None), P("row", "col", None, None), P("row", "col", None))
    n_row, n_col = mesh.shape["row"], mesh.shape["col"]

    def body(*args):
        return local(n_row, n_col, *args)

    return jax.shard_map(body, mesh=mesh, in_specs=in_specs, out_specs=out_specs, check_vma=False)
```

```python
import functools

import jax
import jax.numpy as jnp
from jax import lax
from jax.experimental import pallas as pl
from jax.experimental.pallas import tpu as pltpu
from jax.sharding import PartitionSpec as P


F32 = jnp.float32
BF16 = jnp.bfloat16
HI = lax.Precision.HIGHEST
LANES = 128


def nn(a, b, precision=None):
    return lax.dot_general(
        a, b, (((1,), (0,)), ((), ())), precision=precision, preferred_element_type=F32
    )


def nt(a, b, precision=None):
    return lax.dot_general(
        a, b, (((1,), (1,)), ((), ())), precision=precision, preferred_element_type=F32
    )


def tn(a, b):
    return lax.dot_general(a, b, (((0,), (0,)), ((), ())), preferred_element_type=F32)


def call(kernel, out_shape, *args, hbm=(), raw=(), scratch=()):
    vm, anywhere = pl.BlockSpec(memory_space=pltpu.VMEM), pl.BlockSpec(memory_space=pl.ANY)
    spaces = [pltpu.HBM if k in hbm or k in raw else pltpu.VMEM for k in range(len(args))]
    args = [pltpu.with_memory_space_constraint(x, space) for x, space in zip(args, spaces)]
    return pl.pallas_call(
        kernel,
        out_shape=out_shape,
        in_specs=[anywhere if k in raw else vm for k in range(len(args))],
        out_specs=jax.tree.map(lambda _: vm, out_shape),
        scratch_shapes=list(scratch),
        compiler_params=pltpu.CompilerParams(vmem_limit_bytes=16 << 20),
    )(*args)


def add_all(xs):
    return functools.reduce(lambda a, b: a + b, xs)


def at_block(index, size):
    return pl.ds(pl.multiple_of(index * size, size), size)


def pack_kernel(tiles, rank, cols_ref, vec_ref, u_ref, v_ref):
    chunk, nvec = cols_ref.shape[1], vec_ref.shape[1]
    u = jnp.concatenate([cols_ref[t, :, :rank] for t in range(tiles)], axis=1)
    u_ref[...] = u
    v_ref[:chunk] = jnp.concatenate([cols_ref[t, :, rank:] for t in range(tiles)], axis=1)
    part = nn(vec_ref[...].reshape(tiles * nvec, chunk), u)
    base = chunk
    for b in range(chunk // LANES):
        for t in range(tiles):
            v_ref[base : base + nvec] = vec_ref[t, :, b * LANES : (b + 1) * LANES]
            base += nvec
    part = [part[t * nvec : (t + 1) * nvec, t * rank : (t + 1) * rank] for t in range(tiles)]
    v_ref[base:] = jnp.concatenate(part, axis=1).astype(BF16)


def load_kernel(*refs):
    sources, targets, sems = refs[:4], refs[4:8], refs[8]
    copies = [
        pltpu.make_async_copy(s, t, sems.at[k]) for k, (s, t) in enumerate(zip(sources, targets))
    ]
    for copy in copies:
        copy.start()
    for copy in copies:
        copy.wait()


def coef_kernel(tiles, left, right, omega, psi, coef_a, coef_c):
    for t in range(tiles):
        coef_a[t] = nt(omega[...], right[t]).astype(BF16)
        coef_c[t] = nt(psi[...], left[t]).astype(BF16)


def pair_kernel(own, other, both):
    size = own.shape[0]
    core = lax.axis_index("col") & 1
    both[at_block(core, size), :] = own[...]
    both[at_block(1 - core, size), :] = other[...]


def gram_kernel(tiles, rank, nvec, rparts, cparts, split, ways, *refs):
    left, right = refs[:2]
    rows, refs = refs[2 : 3 + 2 * len(ways)], refs[3 + 2 * len(ways) :]
    vs, gram_out, rows_full = refs[:rparts], refs[rparts], refs[rparts + 1]
    rest, vec_full = refs[rparts + 2 : -1], refs[-1]
    row, col = lax.axis_index("row"), lax.axis_index("col")
    size = rows_full.shape[0] // cparts
    core, chip = col & 1, col >> 1
    rows_full[at_block(chip, 2 * size), :] = rows[0][...]
    for (one, two), mine, other in zip(ways, rows[1::2], rows[2::2]):
        if one == two:
            at = 2 * (chip ^ one)
            rows_full[at_block(at + core, size), :] = mine[...]
            rows_full[at_block(at + 1 - core, size), :] = other[...]
        else:
            rows_full[at_block(chip ^ (one + core * (two - one)), 2 * size), :] = mine[...]
            rows_full[at_block(chip ^ (two + core * (one - two)), 2 * size), :] = other[...]
    chunk = left.shape[2] // rparts
    blocks = chunk // LANES
    wide = tiles * nvec
    for k in range(rparts):
        for b in range(blocks):
            at = chunk + b * wide
            vec_full[:, at_block((row ^ k) * blocks + b, LANES)] = vs[k][at : at + wide]
    gram = add_all(
        [tn(rows_full[at_block(row ^ k, chunk), :], vs[k][:chunk]) for k in range(rparts)]
    )[rank:, :]
    gram_out[...] = gram
    coef_p = [
        nt(vec_full[t * nvec : (t + 1) * nvec], right[t]).astype(BF16) for t in range(tiles)
    ]
    total = add_all([nn(coef_p[t], left[t]) for t in range(tiles)])
    proj = add_all([v[chunk + blocks * wide :].astype(F32) for v in vs])
    coef_q = nt(proj, gram, HI).astype(BF16)
    padded = jnp.concatenate([coef_q, jnp.zeros_like(coef_q)], axis=1)
    total = total - nt(padded, rows_full[...])
    if split:
        keep, send, full = rest
        full[...] = total
        for m in range(cparts // 2):
            keep[m] = full[:, at_block(col ^ (2 * m), size)]
            send[m] = full[:, at_block(col ^ (2 * m + 1), size)].astype(BF16)
    else:
        rest[0][...] = total


def final_kernel(tiles, rank, parts, *refs):
    left, right, omega, psi, coef_a, coef_c, gram, rows_full = refs[:8]
    us = refs[8 : 8 + parts]
    out_first, out_second = refs[8 + parts :]
    row = lax.axis_index("row")
    chunk = us[0].shape[0]
    width = omega.shape[0]
    lane = lax.broadcasted_iota(jnp.int32, (width, tiles * rank), 1)
    gram_all = gram[...]
    row_sketch = nn(psi[...], rows_full[...])[:, :rank]
    coef_d = nn(row_sketch, gram_all, HI)
    sketch = add_all(
        [nn(omega[:, at_block(row ^ k, chunk)], us[k][...]) for k in range(parts)]
    )
    lows, ds = [], []
    for t in range(tiles):
        mine = (lane >= t * rank) & (lane < (t + 1) * rank)
        coef_b = nt(jnp.where(mine, sketch, 0.0), gram_all, HI).astype(BF16)
        lows.append(jnp.concatenate([coef_b, jnp.zeros_like(coef_b)], axis=1))
        ds.append(jnp.where(mine, coef_d, 0.0).astype(BF16))
    low = nt(jnp.concatenate(lows, axis=0), rows_full[...])
    for t in range(tiles):
        first = nn(coef_a[t], left[t])
        out_first[t] = (first - low[t * width : (t + 1) * width]).astype(BF16)
    coefs = jnp.concatenate(ds, axis=0)
    for k in range(parts):
        at = at_block(row ^ k, chunk)
        low = nt(coefs, us[k][...])
        for t in range(tiles):
            second = nn(coef_c[t], right[t, :, at])
            out_second[t, :, at] = (second - low[t * width : (t + 1) * width]).astype(BF16)


def routes(n_col):
    far = list(range(n_col // 2 - 1, 0, -1))
    return [(far[0], far[0])] * (len(far) % 2) + list(
        zip(far[len(far) % 2 :: 2], far[len(far) % 2 + 1 :: 2])
    )


def local(n_row, n_col, tile_left, tile_right, panel_rows, panel_cols, vectors, omega, psi):
    tiles, order, rank = tile_left.shape[1:]
    nvec = vectors.shape[2]
    chunk = panel_cols.shape[1]
    size = panel_rows.shape[1]
    wide = omega.shape[1]
    half = n_col // 2

    def swap(axis, count, value, m):
        return lax.ppermute(value, axis, [(i, i ^ m) for i in range(count)])

    def row_swap(value, m):
        return swap("row", n_row, value, m)

    def col_swap(value, m):
        return swap("col", n_col, value, m)

    left = jnp.swapaxes(tile_left[0], 1, 2)
    right = jnp.swapaxes(tile_right[0], 1, 2)
    vec = jnp.swapaxes(vectors, 1, 2)
    omega_t, psi_t = omega.T, psi.T
    rows = panel_rows[0]
    vmem = pltpu.VMEM

    u, v = call(
        functools.partial(pack_kernel, tiles, rank),
        (
            vmem((chunk, tiles * rank), BF16),
            vmem((chunk + tiles * nvec * chunk // LANES + nvec, tiles * rank), BF16),
        ),
        panel_cols,
        vec,
        hbm=(0, 1),
    )
    sources = (left, right, omega_t, psi_t)
    left, right, omega_t, psi_t = call(
        load_kernel,
        tuple(vmem(x.shape, BF16) for x in sources),
        *sources,
        raw=(0, 1, 2, 3),
        scratch=[pltpu.SemaphoreType.DMA((4,))],
    )
    coef_a, coef_c = call(
        functools.partial(coef_kernel, tiles),
        (vmem((tiles, wide, rank), BF16), vmem((tiles, wide, rank), BF16)),
        left,
        right,
        omega_t,
        psi_t,
    )
    vs = [v] + [row_swap(v, k) for k in range(1, n_row)]
    us = [u] + [row_swap(u, k) for k in range(1, n_row)]
    both = call(pair_kernel, vmem((2 * size, 2 * rank), BF16), rows, col_swap(rows, 1))
    ways = routes(n_col)
    row_parts = [both]
    for one, two in ways:
        perm = [(i, i ^ (2 * (two if i % 2 else one))) for i in range(n_col)]
        got = lax.ppermute(rows if one == two else both, "col", perm)
        row_parts += [got, col_swap(got, 1)]

    split = size % LANES == 0
    outs = (
        vmem((rank, tiles * rank), F32),
        vmem((order, 2 * rank), BF16),
    )
    if split:
        outs += (vmem((half, nvec, size), F32), vmem((half, nvec, size), BF16))
    else:
        outs += (vmem((nvec, order), F32),)
    scratch = [pltpu.VMEM((tiles * nvec, order), BF16)]
    gram, rows_full, *rest = call(
        functools.partial(gram_kernel, tiles, rank, nvec, n_row, n_col, split, ways),
        outs,
        left,
        right,
        *row_parts,
        *vs,
        scratch=([pltpu.VMEM((nvec, order), F32)] if split else []) + scratch,
    )
    if split:
        keep, send = rest
    else:
        col = lax.axis_index("col")
        blocks = rest[0].reshape(nvec, n_col, size).swapaxes(0, 1)
        where = col ^ (2 * jnp.arange(half))
        keep = blocks[where]
        send = blocks[where ^ 1].astype(BF16)
    got = col_swap(send, 1)
    mine = keep[0] + got[0].astype(F32)
    arrived = [col_swap((keep[m] + got[m].astype(F32)).astype(BF16), 2 * m) for m in range(1, half)]
    out_first, out_second = call(
        functools.partial(final_kernel, tiles, rank, n_row),
        (
            jax.ShapeDtypeStruct((tiles, wide, order), BF16),
            jax.ShapeDtypeStruct((tiles, wide, order), BF16),
        ),
        left,
        right,
        omega_t,
        psi_t,
        coef_a,
        coef_c,
        gram,
        rows_full,
        *us,
    )
    for x in arrived:
        mine = mine + x.astype(F32)
    return (
        jnp.swapaxes(out_first, 1, 2)[None],
        jnp.swapaxes(out_second, 1, 2)[None],
        mine.T[None],
    )


def solution(mesh):
    in_specs = (
        P("row", "col", None, None),
        P("row", "col", None, None),
        P("row", "col", None),
        P("col", "row", None),
        P("col", "row", None),
        P(),
        P(),
    )
    out_specs = (P("row", "col", None, None), P("row", "col", None, None), P("row", "col", None))
    n_row, n_col = mesh.shape["row"], mesh.shape["col"]

    def body(*args):
        return local(n_row, n_col, *args)

    return jax.shard_map(body, mesh=mesh, in_specs=in_specs, out_specs=out_specs, check_vma=False)
```
